32 devices in a mesh: rep: 4 (over y, core), shard: 8 (over z, x).
Axes of the slice: x: 2, y: 2, z: 4, core: 2. Of those that a mesh axis runs over, the one named last changes fastest.
Arguments:
- layer_input: bfloat16 [32, 197, 768], P(('rep', 'shard')), may hold values from -6 to 6
- cotangent: bfloat16 [32, 197, 768], P(('rep', 'shard')), may hold values from -6 to 6
- live: int32 [32], P(('rep', 'shard')), may hold values 0 or 1
- first_gain: bfloat16 [768], P('shard'), may hold values from 0.099609375 to 1.8984375
- first_bias: bfloat16 [768], P('shard'), may hold values from -3 to 3
- qkv_weight: bfloat16 [768, 2304], P('shard'), may hold values from -0.21875 to 0.21875
- query_bias: bfloat16 [768], P('shard'), may hold values from -3 to 3
- value_bias: bfloat16 [768], P('shard'), may hold values from -3 to 3
- out_weight: bfloat16 [768, 768], P('shard'), may hold values from -1.5 to 1.5
- out_bias: bfloat16 [768], P('shard'), may hold values from -3 to 3
- second_gain: bfloat16 [768], P('shard'), may hold values from 0.099609375 to 1.8984375
- second_bias: bfloat16 [768], P('shard'), may hold values from -3 to 3
- up_weight: bfloat16 [768, 3072], P('shard'), may hold values from -0.21875 to 0.21875
- up_bias: bfloat16 [3072], P('shard'), may hold values from -3 to 3
- down_weight: bfloat16 [3072, 768], P('shard'), may hold values from -0.109375 to 0.109375
- down_bias: bfloat16 [768], P('shard'), may hold values from -3 to 3
Outputs:
- output: bfloat16 [32, 197, 768], P(('rep', 'shard'))
- input_grad: bfloat16 [32, 197, 768], P(('rep', 'shard'))
- first_gain_grad: float32 [768], P('shard')
- first_bias_grad: float32 [768], P('shard')
- qkv_weight_grad: float32 [768, 2304], P('shard')
- query_bias_grad: float32 [768], P('shard')
- value_bias_grad: float32 [768], P('shard')
- out_weight_grad: float32 [768, 768], P('shard')
- out_bias_grad: float32 [768], P('shard')
- second_gain_grad: float32 [768], P('shard')
- second_bias_grad: float32 [768], P('shard')
- up_weight_grad: float32 [768, 3072], P('shard')
- up_bias_grad: float32 [3072], P('shard')
- down_weight_grad: float32 [3072, 768], P('shard')
- down_bias_grad: float32 [768], P('shard')
The draws below stay inside these ranges and needn't reach their ends.
All inputs are finite; a program needn't handle non-finite values. No bound on the sum of `live` on one device may be relied on, other than what follows from the above.
Results may differ from the reference program's by a relative error of at most 0.014.
Values may be sent and summed in bfloat16 or wider, within the bound.
A program may use at most 128 MiB of HBM per device.

```python
import jax
import jax.numpy as jnp
from jax import lax

D = 768
FF = 3072
HEAD_DIM = 64
SEQ = 197
IMAGES = 32


def set_ends(values, own_key, smallest, top_value):
    extent = values.shape
    place = [jax.random.randint(jax.random.fold_in(own_key, axis), (), 0, extent[axis]) for axis in range(len(extent))]
    values = values.at[tuple(place)].set(smallest)
    longest = extent.index(max(extent))
    place[longest] = (place[longest] + 1) % extent[longest]
    return values.at[tuple(place)].set(top_value)


def level_of(own_key, dims, pieces, low, largest):
    gain = 1.0
    for dim, parts in pieces:
        draws = jax.random.uniform(jax.random.fold_in(jax.random.fold_in(own_key, 6), dim), (parts,), jnp.float32, low / len(pieces), largest / len(pieces))
        gain = gain * jnp.repeat(jnp.exp(draws), dims[dim] // parts).reshape((-1,) + (1,) * (len(dims) - 1 - dim))
    return gain


def gaussian(key, extent, scale, bound, shards=(), held_as=jnp.bfloat16):
    entries = scale * jax.random.normal(key, extent, jnp.float32)
    if shards:
        entries = entries * level_of(key, extent, shards, -0.22, 0.18)
    return jnp.clip(entries, -bound, bound).astype(held_as)


def setup_inputs(seed: int = 0) -> dict:
    key_of = jax.random.split(jax.random.key(seed), 17)
    return {
        "layer_input": gaussian(key_of[0], (IMAGES, SEQ, D), 1.0, 6.0, ((0, 32),)),
        "cotangent": gaussian(key_of[1], (IMAGES, SEQ, D), 1.0, 6.0, ((0, 32),)),
        "live": set_ends((jax.random.randint(key_of[2], (IMAGES,), 0, 4) < 3).astype(jnp.int32), jax.random.fold_in(key_of[2], 1), 0, 1),
        "first_gain": jnp.clip(1.0 + 0.18 * jax.random.normal(key_of[3], (D,), jnp.float32), 0.099609375, 1.8984375).astype(jnp.bfloat16),
        "first_bias": gaussian(key_of[4], (D,), 0.5, 3.0, ((0, 8),)),
        "qkv_weight": gaussian(key_of[5], (D, 3 * D), D ** -0.5, 0.21875, ((0, 8),)),
        "query_bias": gaussian(key_of[6], (D,), 0.5, 3.0, ((0, 8),)),
        "value_bias": gaussian(key_of[7], (D,), 0.5, 3.0, ((0, 8),)),
        "out_weight": gaussian(key_of[8], (D, D), (D // 48) ** -0.5, 1.5, ((0, 8),)),
        "out_bias": gaussian(key_of[9], (D,), 0.5, 3.0, ((0, 8),)),
        "second_gain": jnp.clip(1.0 + 0.18 * jax.random.normal(key_of[10], (D,), jnp.float32), 0.099609375, 1.8984375).astype(jnp.bfloat16),
        "second_bias": gaussian(key_of[11], (D,), 0.5, 3.0, ((0, 8),)),
        "up_weight": gaussian(key_of[12], (D, FF), D ** -0.5, 0.21875, ((0, 8),)),
        "up_bias": gaussian(key_of[13], (FF,), 0.5, 3.0, ((0, 8),)),
        "down_weight": gaussian(key_of[14], (FF, D), FF ** -0.5, 0.109375, ((0, 8),)),
        "down_bias": gaussian(key_of[15], (D,), 0.5, 3.0, ((0, 8),)),
    }


norm_eps = 1e-06
root_half = 0.7071067811865476
density_coef = 0.3989422804014327

def matmul(operand, factor):
    flat = operand.reshape(-1, operand.shape[-1])
    product = jnp.dot(flat, factor, preferred_element_type=jnp.float32)
    return product.reshape(operand.shape[:-1] + (factor.shape[-1],))

def outer_product(operand, factor):
    return jnp.dot(operand.reshape(-1, operand.shape[-1]).T, factor.reshape(-1, factor.shape[-1]), preferred_element_type=jnp.float32)

def batched(form, operand, factor):
    return jnp.einsum(form, operand.astype(jnp.float32), factor.astype(jnp.float32))

def layer_norm(values, norm_gain, norm_bias):
    average = lax.optimization_barrier(jnp.mean(values, axis=-1, keepdims=True))
    centred = values - average
    spread = lax.optimization_barrier(jnp.mean(centred * centred, axis=-1, keepdims=True))
    inv_std = lax.rsqrt(spread + norm_eps)
    hat_vals = centred * inv_std
    return (hat_vals * norm_gain.astype(jnp.float32) + norm_bias.astype(jnp.float32), hat_vals, inv_std)

def norm_back(incoming, hat_vals, inv_std, norm_gain):
    scaled = incoming * norm_gain.astype(jnp.float32)
    return inv_std * (scaled - lax.optimization_barrier(jnp.mean(scaled, axis=-1, keepdims=True)) - hat_vals * lax.optimization_barrier(jnp.mean(scaled * hat_vals, axis=-1, keepdims=True)))

def block_pass(params, layer_input, cotangent, live):
    first_gain, first_bias, qkv_weight, query_bias, value_bias, out_weight, out_bias, second_gain, second_bias, up_weight, up_bias, down_weight, down_bias = params
    images, length, model_width = layer_input.shape
    head_count = model_width // HEAD_DIM
    score_scale = HEAD_DIM ** (-0.5)
    stream = layer_input.astype(jnp.float32)
    normed, first_hat, first_inv = layer_norm(stream, first_gain, first_bias)
    normed = normed.astype(jnp.bfloat16)
    projected = matmul(normed, qkv_weight)
    shape_heads = (images, length, head_count, HEAD_DIM)
    queries = (projected[..., :model_width] + query_bias.astype(jnp.float32)).astype(jnp.bfloat16).reshape(shape_heads)
    key_rows = projected[..., model_width:2 * model_width].astype(jnp.bfloat16).reshape(shape_heads)
    values = (projected[..., 2 * model_width:] + value_bias.astype(jnp.float32)).astype(jnp.bfloat16).reshape(shape_heads)
    scores = batched('bqhd,bkhd->bhqk', queries, key_rows) * score_scale
    log_total = jnp.log(lax.optimization_barrier(jnp.sum(jnp.exp(scores), axis=-1, keepdims=True)))
    weights = jnp.exp(scores - log_total).astype(jnp.bfloat16)
    attended = batched('bhqk,bkhd->bqhd', weights, values).reshape(images, length, model_width).astype(jnp.bfloat16)
    middle = stream + matmul(attended, out_weight) + out_bias.astype(jnp.float32)
    second_normed, second_hat, second_inv = layer_norm(middle, second_gain, second_bias)
    second_normed = second_normed.astype(jnp.bfloat16)
    hidden_pre = matmul(second_normed, up_weight) + up_bias.astype(jnp.float32)
    normal_cdf = 0.5 * (1.0 + lax.erf(hidden_pre * root_half))
    hidden = (hidden_pre * normal_cdf).astype(jnp.bfloat16)
    result = middle + matmul(hidden, down_weight) + down_bias.astype(jnp.float32)
    image_mask = live.astype(jnp.float32)[:, None, None]
    output = (result * image_mask).astype(jnp.bfloat16)
    upstream = cotangent.astype(jnp.float32) * image_mask
    upstream_low = upstream.astype(jnp.bfloat16)
    down_weight_grad = outer_product(hidden, upstream_low)
    down_bias_grad = lax.optimization_barrier(jnp.sum(upstream, axis=(0, 1)))
    hidden_grad = matmul(upstream_low, down_weight.T)
    density = jnp.exp(-0.5 * hidden_pre * hidden_pre) * density_coef
    pre_grad = hidden_grad * (normal_cdf + hidden_pre * density)
    pre_low = pre_grad.astype(jnp.bfloat16)
    up_weight_grad = outer_product(second_normed, pre_low)
    up_bias_grad = lax.optimization_barrier(jnp.sum(pre_grad, axis=(0, 1)))
    second_in = matmul(pre_low, up_weight.T)
    second_gain_grad = lax.optimization_barrier(jnp.sum(second_in * second_hat, axis=(0, 1)))
    second_bias_grad = lax.optimization_barrier(jnp.sum(second_in, axis=(0, 1)))
    middle_grad = upstream + norm_back(second_in, second_hat, second_inv, second_gain)
    middle_low = middle_grad.astype(jnp.bfloat16)
    out_weight_grad = outer_product(attended, middle_low)
    out_bias_grad = lax.optimization_barrier(jnp.sum(middle_grad, axis=(0, 1)))
    attended_grad = matmul(middle_low, out_weight.T).astype(jnp.bfloat16).reshape(shape_heads)
    again_scores = batched('bqhd,bkhd->bhqk', queries, key_rows) * score_scale
    probs = jnp.exp(again_scores - log_total)
    probs_low = probs.astype(jnp.bfloat16)
    value_grad = batched('bhqk,bqhd->bkhd', probs_low, attended_grad)
    prob_grad = batched('bqhd,bkhd->bhqk', attended_grad, values)
    score_grad = (probs * (prob_grad - lax.optimization_barrier(jnp.sum(probs * prob_grad, axis=-1, keepdims=True))) * score_scale).astype(jnp.bfloat16)
    query_grad = batched('bhqk,bkhd->bqhd', score_grad, key_rows)
    key_grad = batched('bhqk,bqhd->bkhd', score_grad, queries)
    flat_shape = (images, length, model_width)
    query_grad = query_grad.reshape(flat_shape)
    value_grad = value_grad.reshape(flat_shape)
    joined = jnp.concatenate([query_grad, key_grad.reshape(flat_shape), value_grad], axis=-1).astype(jnp.bfloat16)
    qkv_weight_grad = outer_product(normed, joined)
    query_bias_grad = lax.optimization_barrier(jnp.sum(query_grad, axis=(0, 1)))
    value_bias_grad = lax.optimization_barrier(jnp.sum(value_grad, axis=(0, 1)))
    first_in = matmul(joined, qkv_weight.T)
    first_gain_grad = lax.optimization_barrier(jnp.sum(first_in * first_hat, axis=(0, 1)))
    first_bias_grad = lax.optimization_barrier(jnp.sum(first_in, axis=(0, 1)))
    input_grad = (middle_grad + norm_back(first_in, first_hat, first_inv, first_gain)).astype(jnp.bfloat16)
    grads = (first_gain_grad, first_bias_grad, qkv_weight_grad, query_bias_grad, value_bias_grad, out_weight_grad, out_bias_grad, second_gain_grad, second_bias_grad, up_weight_grad, up_bias_grad, down_weight_grad, down_bias_grad)
    return (output, input_grad, grads)

def reference(layer_input, cotangent, live, first_gain, first_bias, qkv_weight, query_bias, value_bias, out_weight, out_bias, second_gain, second_bias, up_weight, up_bias, down_weight, down_bias):
    params = (first_gain, first_bias, qkv_weight, query_bias, value_bias, out_weight, out_bias, second_gain, second_bias, up_weight, up_bias, down_weight, down_bias)
    blocks = IMAGES // 16
    inputs_blocked = layer_input.reshape(blocks, 16, SEQ, D)
    cot_blocked = cotangent.reshape(blocks, 16, SEQ, D)
    live_blocked = live.reshape(blocks, 16)

    def advance(totals, item):
        output, input_grad, grads = block_pass(params, item[0], item[1], item[2])
        return (tuple((total + grad for total, grad in zip(totals, grads))), (output, input_grad))
    zeros = tuple((jnp.zeros(param.shape, jnp.float32) for param in params))
    totals, (outputs, input_grads) = lax.scan(advance, zeros, (inputs_blocked, cot_blocked, live_blocked))
    return (outputs.reshape(IMAGES, SEQ, D), input_grads.reshape(IMAGES, SEQ, D), totals[0], totals[1], totals[2], totals[3], totals[4], totals[5], totals[6], totals[7], totals[8], totals[9], totals[10], totals[11], totals[12])
```

```python
import functools

import jax
import jax.numpy as jnp
from jax import lax
from jax.experimental import pallas as pl
from jax.experimental.pallas import tpu as pltpu
from jax.sharding import PartitionSpec as P

HEAD_DIM = 64


norm_eps = 1e-06
root_half = 0.7071067811865476
density_coef = 0.3989422804014327


def matmul(operand, factor):
    flat = operand.reshape(-1, operand.shape[-1])
    product = jnp.dot(flat, factor, preferred_element_type=jnp.float32)
    return product.reshape(operand.shape[:-1] + (factor.shape[-1],))


def outer_product(operand, factor):
    return jnp.dot(
        operand.reshape(-1, operand.shape[-1]).T,
        factor.reshape(-1, factor.shape[-1]),
        preferred_element_type=jnp.float32,
    )


def batched(form, operand, factor):
    return jnp.einsum(form, operand, factor, preferred_element_type=jnp.float32)


def layer_norm(values, norm_gain, norm_bias):
    average = jnp.mean(values, axis=-1, keepdims=True)
    centred = values - average
    spread = jnp.mean(centred * centred, axis=-1, keepdims=True)
    inv_std = lax.rsqrt(spread + norm_eps)
    hat_vals = centred * inv_std
    return (
        hat_vals * norm_gain.astype(jnp.float32) + norm_bias.astype(jnp.float32),
        hat_vals,
        inv_std,
    )


def norm_back(incoming, hat_vals, inv_std, norm_gain):
    scaled = incoming * norm_gain.astype(jnp.float32)
    return inv_std * (
        scaled
        - jnp.mean(scaled, axis=-1, keepdims=True)
        - hat_vals * jnp.mean(scaled * hat_vals, axis=-1, keepdims=True)
    )


def forward_pass(params, layer_input, live):
    (
        first_gain,
        first_bias,
        qkv_weight,
        query_bias,
        value_bias,
        out_weight,
        out_bias,
        second_gain,
        second_bias,
        up_weight,
        up_bias,
        down_weight,
        down_bias,
    ) = params
    images, length, model_width = layer_input.shape
    head_count = model_width // HEAD_DIM
    score_scale = HEAD_DIM ** (-0.5)
    stream = layer_input.astype(jnp.float32)
    normed, first_hat, first_inv = layer_norm(stream, first_gain, first_bias)
    normed = normed.astype(jnp.bfloat16)
    projected = matmul(normed, qkv_weight)
    shape_heads = (images, length, head_count, HEAD_DIM)
    queries = (
        (projected[..., :model_width] + query_bias.astype(jnp.float32))
        .astype(jnp.bfloat16)
        .reshape(shape_heads)
    )
    key_rows = (
        projected[..., model_width : 2 * model_width].astype(jnp.bfloat16).reshape(shape_heads)
    )
    values = (
        (projected[..., 2 * model_width :] + value_bias.astype(jnp.float32))
        .astype(jnp.bfloat16)
        .reshape(shape_heads)
    )
    scores = batched("bqhd,bkhd->bhqk", queries, key_rows) * score_scale
    log_total = jnp.log(jnp.sum(jnp.exp(scores), axis=-1, keepdims=True))
    weights = jnp.exp(scores - log_total).astype(jnp.bfloat16)
    attended = (
        batched("bhqk,bkhd->bqhd", weights, values)
        .reshape(images, length, model_width)
        .astype(jnp.bfloat16)
    )
    middle = stream + matmul(attended, out_weight) + out_bias.astype(jnp.float32)
    second_normed, second_hat, second_inv = layer_norm(middle, second_gain, second_bias)
    second_normed = second_normed.astype(jnp.bfloat16)
    hidden_pre = matmul(second_normed, up_weight) + up_bias.astype(jnp.float32)
    normal_cdf = 0.5 * (1.0 + lax.erf(hidden_pre * root_half))
    hidden = (hidden_pre * normal_cdf).astype(jnp.bfloat16)
    result = middle + matmul(hidden, down_weight) + down_bias.astype(jnp.float32)
    image_mask = live.astype(jnp.float32)[:, None, None]
    output = (result * image_mask).astype(jnp.bfloat16)
    saved = (
        normed,
        first_hat,
        first_inv,
        queries,
        key_rows,
        values,
        log_total,
        attended,
        second_normed,
        second_hat,
        second_inv,
        hidden_pre,
        normal_cdf,
        hidden,
        image_mask,
    )
    return (output, saved)


def backward_pass(params, saved, cotangent):
    (
        first_gain,
        first_bias,
        qkv_weight,
        query_bias,
        value_bias,
        out_weight,
        out_bias,
        second_gain,
        second_bias,
        up_weight,
        up_bias,
        down_weight,
        down_bias,
    ) = params
    (
        normed,
        first_hat,
        first_inv,
        queries,
        key_rows,
        values,
        log_total,
        attended,
        second_normed,
        second_hat,
        second_inv,
        hidden_pre,
        normal_cdf,
        hidden,
        image_mask,
    ) = saved
    images, length, head_count, head_width = queries.shape
    flat_shape = (images, length, head_count * head_width)
    score_scale = HEAD_DIM ** (-0.5)
    upstream = cotangent.astype(jnp.float32) * image_mask
    upstream_low = upstream.astype(jnp.bfloat16)
    down_weight_grad = outer_product(hidden, upstream_low)
    down_bias_grad = jnp.sum(upstream, axis=(0, 1))
    hidden_grad = matmul(upstream_low, down_weight.T)
    density = jnp.exp(-0.5 * hidden_pre * hidden_pre) * density_coef
    pre_grad = hidden_grad * (normal_cdf + hidden_pre * density)
    pre_low = pre_grad.astype(jnp.bfloat16)
    up_weight_grad = outer_product(second_normed, pre_low)
    up_bias_grad = jnp.sum(pre_grad, axis=(0, 1))
    second_in = matmul(pre_low, up_weight.T)
    second_gain_grad = jnp.sum(second_in * second_hat, axis=(0, 1))
    second_bias_grad = jnp.sum(second_in, axis=(0, 1))
    middle_grad = upstream + norm_back(second_in, second_hat, second_inv, second_gain)
    middle_low = middle_grad.astype(jnp.bfloat16)
    out_weight_grad = outer_product(attended, middle_low)
    out_bias_grad = jnp.sum(middle_grad, axis=(0, 1))
    attended_grad = matmul(middle_low, out_weight.T).astype(jnp.bfloat16).reshape(queries.shape)
    again_scores = batched("bqhd,bkhd->bhqk", queries, key_rows) * score_scale
    probs = jnp.exp(again_scores - log_total)
    probs_low = probs.astype(jnp.bfloat16)
    value_grad = batched("bhqk,bqhd->bkhd", probs_low, attended_grad)
    prob_grad = batched("bqhd,bkhd->bhqk", attended_grad, values)
    score_grad = (
        probs * (prob_grad - jnp.sum(probs * prob_grad, axis=-1, keepdims=True)) * score_scale
    ).astype(jnp.bfloat16)
    query_grad = batched("bhqk,bkhd->bqhd", score_grad, key_rows).reshape(flat_shape)
    key_grad = batched("bhqk,bqhd->bkhd", score_grad, queries).reshape(flat_shape)
    value_grad = value_grad.reshape(flat_shape)
    joined = jnp.concatenate([query_grad, key_grad, value_grad], axis=-1).astype(jnp.bfloat16)
    qkv_weight_grad = outer_product(normed, joined)
    query_bias_grad = jnp.sum(query_grad, axis=(0, 1))
    value_bias_grad = jnp.sum(value_grad, axis=(0, 1))
    first_in = matmul(joined, qkv_weight.T)
    first_gain_grad = jnp.sum(first_in * first_hat, axis=(0, 1))
    first_bias_grad = jnp.sum(first_in, axis=(0, 1))
    middle_grad = middle_grad + norm_back(first_in, first_hat, first_inv, first_gain)
    input_grad = middle_grad.astype(jnp.bfloat16)
    grads = (
        first_gain_grad,
        first_bias_grad,
        qkv_weight_grad,
        query_bias_grad,
        value_bias_grad,
        out_weight_grad,
        out_bias_grad,
        second_gain_grad,
        second_bias_grad,
        up_weight_grad,
        up_bias_grad,
        down_weight_grad,
        down_bias_grad,
    )
    return (input_grad, grads)


MESH = pl.DeviceIdType.MESH
UNIT = 16


def ring_index(position, n):
    half = position // (n // 2)
    return (1 - half) * 2 * position + half * (2 * (n - 1 - position) + 1)


def ring_position(index, n):
    odd = index % 2
    step = index // 2
    return (1 - odd) * step + odd * (n - 1 - step)


def make_streams(half_rows, n):
    units = half_rows // UNIT
    per_way = 2 if n <= 16 else 1
    count = min(2 * per_way, units)
    edges = [units * i // count for i in range(count + 1)]
    return [
        (1 if 2 * i < count else -1, edges[i] * UNIT, (edges[i + 1] - edges[i]) * UNIT)
        for i in range(count)
    ]


def places(n):
    rep = lax.axis_index("rep")
    me = lax.axis_index("shard")
    core = rep % 2
    row = rep // 2
    position = ring_position(me, n)
    right = (rep, ring_index((position + 1) % n, n))
    left = (rep, ring_index((position + n - 1) % n, n))
    partner = (row * 2 + 1 - core, me)
    across = ((1 - row) * 2 + core, me)
    return me, core, row, position, right, left, partner, across


def greet(peers):
    barrier = pltpu.get_barrier_semaphore()
    for peer in peers:
        pl.semaphore_signal(barrier, inc=1, device_id=peer, device_id_type=MESH)
    pl.semaphore_wait(barrier, len(peers))


def remote(source, target, send, recv, device):
    return pltpu.make_async_remote_copy(
        src_ref=source,
        dst_ref=target,
        send_sem=send,
        recv_sem=recv,
        device_id=device,
        device_id_type=MESH,
    )


def gather_kernel(
    n,
    half,
    streams,
    in_ref,
    out_ref,
    local_sem,
    ring_s,
    ring_r,
    core_s,
    core_r,
    row_s,
    row_r,
    last_s,
    last_r,
):
    me, core, row, position, right, left, partner, across = places(n)
    own = pltpu.make_async_copy(in_ref, out_ref.at[me], local_sem)
    own.start()
    greet((right, left, partner, across))
    own.wait()

    def third(size):
        return (size // UNIT // 3) * UNIT

    def block(i, r):
        sign = streams[i][0]
        return ring_index((position + (n - sign) * r) % n, n)

    def window(i, r, base, start, size):
        first = pl.multiple_of(base * half + start, UNIT)
        return out_ref.at[block(i, r), pl.ds(first, size)]

    def ring(i, r):
        sign, start, size = streams[i]
        cut = third(size)
        part = window(i, r, core, start + row * cut, size - cut)
        return remote(part, part, ring_s.at[i, r], ring_r.at[i, r], right if sign > 0 else left)

    def to_core(i, r, base):
        sign, start, size = streams[i]
        cut = third(size)
        part = window(i, r + 1, base, start + row * cut, size - cut)
        return remote(part, part, core_s.at[i, r], core_r.at[i, r], partner)

    def to_row(i, r, which):
        sign, start, size = streams[i]
        cut = third(size)
        part = window(i, r + 1, core, start + which * (size - cut), cut)
        return remote(part, part, row_s.at[i, r], row_r.at[i, r], across)

    def to_last(i, r, base):
        sign, start, size = streams[i]
        cut = third(size)
        part = window(i, r + 1, base, start + (1 - row) * (size - cut), cut)
        return remote(part, part, last_s.at[i, r], last_r.at[i, r], partner)

    every = range(len(streams))
    split = [i for i in every if third(streams[i][2]) > 0]

    def arrived(i, r):
        sign, start, size = streams[i]
        cut = third(size)
        part = window(i, r + 1, core, start + row * cut, size - cut)
        return remote(part, part, ring_s.at[i, r], ring_r.at[i, r], right if sign > 0 else left)

    for i in every:
        ring(i, 0).start()

    def relay(r):
        for i in split:
            to_row(i, r, 1 - row).wait_recv()
            to_last(i, r, core).start()

    def step(r, carry):
        for i in every:
            arrived(i, r).wait_recv()

            @pl.when(r < n - 2)
            def _():
                ring(i, r + 1).start()

            if third(streams[i][2]) > 0:
                to_row(i, r, row).start()
            to_core(i, r, core).start()

        @pl.when(r > 0)
        def _():
            relay(r - 1)

        return carry

    lax.fori_loop(0, n - 1, step, 0)
    relay(n - 2)

    def finish(r, carry):
        for i in every:
            ring(i, r).wait_send()
            to_core(i, r, core).wait_send()
            to_core(i, r, 1 - core).wait_recv()
        for i in split:
            to_row(i, r, row).wait_send()
            to_last(i, r, core).wait_send()
            to_last(i, r, 1 - core).wait_recv()
        return carry

    lax.fori_loop(0, n - 1, finish, 0)


def gather_all(packed, n):
    rows, width = packed.shape
    half = rows // 2
    streams = make_streams(half, n)
    sems = pltpu.SemaphoreType.DMA((len(streams), n - 1))
    return pl.pallas_call(
        functools.partial(gather_kernel, n, half, streams),
        out_shape=jax.ShapeDtypeStruct((n, rows, width), packed.dtype),
        in_specs=[pl.BlockSpec(memory_space=pltpu.VMEM)],
        out_specs=pl.BlockSpec(memory_space=pl.ANY),
        scratch_shapes=[pltpu.SemaphoreType.DMA] + [sems] * 8,
        compiler_params=pltpu.CompilerParams(collective_id=0, has_side_effects=True),
        name="gather_all",
    )(packed)


def reduce_kernel(
    n,
    half,
    streams,
    in_ref,
    out_ref,
    own,
    given,
    arrive,
    other,
    own_sem,
    given_s,
    given_r,
    ring_s,
    ring_r,
    row_s,
    row_r,
    core_s,
    core_r,
):
    me, core, row, position, right, left, partner, across = places(n)
    every = range(len(streams))

    def source(i, k, base):
        sign, start, size = streams[i]
        index = ring_index((position + (n - sign) * (k + 1)) % n, n)
        first = pl.multiple_of(base * half + start, UNIT)
        return in_ref.at[index, pl.ds(first, size)]

    def part(ref, i, k):
        sign, start, size = streams[i]
        return ref.at[k, pl.ds(start, size)]

    def load(i, k):
        return pltpu.make_async_copy(source(i, k, core), part(own, i, k), own_sem.at[i, k])

    def give(i, k):
        return remote(
            source(i, k, 1 - core), part(given, i, k), given_s.at[i, k], given_r.at[i, k], partner
        )

    def ring(i, k):
        return remote(
            part(own, i, k),
            part(arrive, i, k),
            ring_s.at[i, k],
            ring_r.at[i, k],
            right if streams[i][0] > 0 else left,
        )

    def loads(k, carry):
        for i in every:
            load(i, k).start()
        return carry

    lax.fori_loop(0, n, loads, 0)
    greet((right, left, partner, across))

    def gives(k, carry):
        for i in every:
            give(i, k).start()
        return carry

    lax.fori_loop(0, n, gives, 0)

    def take(i, k):
        load(i, k).wait()
        give(i, k).wait_recv()
        sign, start, size = streams[i]
        rows = pl.ds(start, size)
        return own[k, rows].astype(jnp.float32) + given[k, rows].astype(jnp.float32)

    def put(i, k, total):
        sign, start, size = streams[i]
        own[k, pl.ds(start, size)] = total.astype(own.dtype)

    for i in every:
        put(i, 0, take(i, 0))
        ring(i, 0).start()

    def step(k, carry):
        for i in every:
            sign, start, size = streams[i]
            total = take(i, k)
            ring(i, k - 1).wait_recv()
            put(i, k, total + arrive[k - 1, pl.ds(start, size)].astype(jnp.float32))
            ring(i, k).start()
        return carry

    lax.fori_loop(1, n - 1, step, 0)

    def to_row(i):
        sign, start, size = streams[i]
        return remote(
            part(own, i, n - 1),
            other.at[pl.ds(start, size)],
            row_s.at[i],
            row_r.at[i],
            across,
        )

    def to_core(i, base):
        sign, start, size = streams[i]
        block = out_ref.at[base, pl.ds(start, size)]
        return remote(block, block, core_s.at[i], core_r.at[i], partner)

    for i in every:
        sign, start, size = streams[i]
        total = take(i, n - 1)
        ring(i, n - 2).wait_recv()
        put(i, n - 1, total + arrive[n - 2, pl.ds(start, size)].astype(jnp.float32))
        to_row(i).start()
    for i in every:
        sign, start, size = streams[i]
        rows = pl.ds(start, size)
        to_row(i).wait_recv()
        total = own[n - 1, rows].astype(jnp.float32) + other[rows].astype(jnp.float32)
        out_ref[core, rows] = total.astype(out_ref.dtype)
        to_core(i, core).start()
    for i in every:
        to_row(i).wait_send()
        to_core(i, core).wait_send()
        to_core(i, 1 - core).wait_recv()

    def finish(k, carry):
        for i in every:
            give(i, k).wait_send()
        return carry

    lax.fori_loop(0, n, finish, 0)

    def finish_ring(k, carry):
        for i in every:
            ring(i, k).wait_send()
        return carry

    lax.fori_loop(0, n - 1, finish_ring, 0)


def reduce_all(blocks):
    n, rows, width = blocks.shape
    half = rows // 2
    streams = make_streams(half, n)
    count = len(streams)
    dma = pltpu.SemaphoreType.DMA
    low = blocks.dtype
    return pl.pallas_call(
        functools.partial(reduce_kernel, n, half, streams),
        out_shape=jax.ShapeDtypeStruct((2, half, width), low),
        in_specs=[pl.BlockSpec(memory_space=pl.ANY)],
        out_specs=pl.BlockSpec(memory_space=pltpu.VMEM),
        scratch_shapes=[
            pltpu.VMEM((n, half, width), low),
            pltpu.VMEM((n, half, width), low),
            pltpu.VMEM((n - 1, half, width), low),
            pltpu.VMEM((half, width), low),
            dma((count, n)),
            dma((count, n)),
            dma((count, n)),
            dma((count, n - 1)),
            dma((count, n - 1)),
            dma((count,)),
            dma((count,)),
            dma((count,)),
            dma((count,)),
        ],
        compiler_params=pltpu.CompilerParams(
            collective_id=1, has_side_effects=True, vmem_limit_bytes=48 * 1024 * 1024
        ),
        name="reduce_all",
    )(blocks).reshape(rows, width)


def per_device(n, layer_input, cotangent, live, *params):
    width = params[0].shape[0] * n
    matrices = [i for i, p in enumerate(params) if p.ndim == 2]
    vectors = [i for i, p in enumerate(params) if p.ndim == 1]

    pieces, place, row = [], {}, 0
    for i in matrices:
        rows, columns = params[i].shape
        place[i] = []
        for c in range(columns // width):
            pieces.append(params[i][:, c * width : (c + 1) * width])
            place[i].append(row)
            row += rows
    lengths = [params[i].shape[0] for i in vectors]
    total = -(-(row * width + sum(lengths)) // (2 * UNIT * width)) * 2 * UNIT
    spare = (total - row) * width - sum(lengths)
    line = jnp.concatenate([params[i] for i in vectors] + [jnp.zeros(spare, params[0].dtype)])
    pieces.append(line.reshape(total - row, width))
    everything = gather_all(jnp.concatenate(pieces, axis=0), n)

    gathered = [None] * len(params)
    for i in matrices:
        rows = params[i].shape[0]
        gathered[i] = jnp.concatenate(
            [everything[:, r : r + rows].reshape(n * rows, width) for r in place[i]], axis=1
        )
    tail = everything[:, row:].reshape(n, -1)
    at = 0
    for i, length in zip(vectors, lengths):
        gathered[i] = tail[:, at : at + length].reshape(-1)
        at += length

    output, saved = forward_pass(gathered, layer_input, live)
    input_grad, grads = backward_pass(gathered, saved, cotangent)

    low = jnp.bfloat16
    blocks = []
    for i in matrices:
        rows, columns = params[i].shape
        grad = grads[i].astype(low)
        for c in range(columns // width):
            blocks.append(grad[:, c * width : (c + 1) * width].reshape(n, rows, width))
    lines = [grads[i].astype(low).reshape(n, -1) for i in vectors] + [jnp.zeros((n, spare), low)]
    blocks.append(jnp.concatenate(lines, axis=1).reshape(n, total - row, width))
    summed = reduce_all(jnp.concatenate(blocks, axis=1))

    results = [None] * len(params)
    for i in matrices:
        rows = params[i].shape[0]
        results[i] = jnp.concatenate([summed[r : r + rows] for r in place[i]], axis=1).astype(
            jnp.float32
        )
    tail = summed[row:].reshape(-1)
    at = 0
    for i, length in zip(vectors, lengths):
        results[i] = tail[at : at + length].astype(jnp.float32)
        at += length
    return (output, input_grad, *results)


def solution(mesh):
    placed = (
        P(("rep", "shard"), None, None),
        P(("rep", "shard"), None, None),
        P(("rep", "shard")),
        P("shard"),
        P("shard"),
        P("shard", None),
        P("shard"),
        P("shard"),
        P("shard", None),
        P("shard"),
        P("shard"),
        P("shard"),
        P("shard", None),
        P("shard"),
        P("shard", None),
        P("shard"),
    )
    return jax.shard_map(
        functools.partial(per_device, mesh.shape["shard"]),
        mesh=mesh,
        in_specs=placed,
        out_specs=(
            P(("rep", "shard"), None, None),
            P(("rep", "shard"), None, None),
            P("shard"),
            P("shard"),
            P("shard", None),
            P("shard"),
            P("shard"),
            P("shard", None),
            P("shard"),
            P("shard"),
            P("shard"),
            P("shard", None),
            P("shard"),
            P("shard", None),
            P("shard"),
        ),
        check_vma=False,
    )
```

```python
import functools

import jax
import jax.numpy as jnp
from jax import lax
from jax.experimental import pallas as pl
from jax.experimental.pallas import tpu as pltpu
from jax.sharding import PartitionSpec as P

HEAD_DIM = 64


norm_eps = 1e-06
root_half = 0.7071067811865476
density_coef = 0.3989422804014327


def matmul(operand, factor):
    flat = operand.reshape(-1, operand.shape[-1])
    product = jnp.dot(flat, factor, preferred_element_type=jnp.float32)
    return product.reshape(operand.shape[:-1] + (factor.shape[-1],))


def outer_product(operand, factor):
    return jnp.dot(
        operand.reshape(-1, operand.shape[-1]).T,
        factor.reshape(-1, factor.shape[-1]),
        preferred_element_type=jnp.float32,
    )


def batched(form, operand, factor):
    return jnp.einsum(form, operand, factor, preferred_element_type=jnp.float32)


def layer_norm(values, norm_gain, norm_bias):
    average = jnp.mean(values, axis=-1, keepdims=True)
    centred = values - average
    spread = jnp.mean(centred * centred, axis=-1, keepdims=True)
    inv_std = lax.rsqrt(spread + norm_eps)
    hat_vals = centred * inv_std
    return (
        hat_vals * norm_gain.astype(jnp.float32) + norm_bias.astype(jnp.float32),
        hat_vals,
        inv_std,
    )


def norm_back(incoming, hat_vals, inv_std, norm_gain):
    scaled = incoming * norm_gain.astype(jnp.float32)
    return inv_std * (
        scaled
        - jnp.mean(scaled, axis=-1, keepdims=True)
        - hat_vals * jnp.mean(scaled * hat_vals, axis=-1, keepdims=True)
    )


def forward_pass(params, layer_input, live):
    (
        first_gain,
        first_bias,
        qkv_weight,
        query_bias,
        value_bias,
        out_weight,
        out_bias,
        second_gain,
        second_bias,
        up_weight,
        up_bias,
        down_weight,
        down_bias,
    ) = params
    images, length, model_width = layer_input.shape
    head_count = model_width // HEAD_DIM
    score_scale = HEAD_DIM ** (-0.5)
    stream = layer_input.astype(jnp.float32)
    normed, first_hat, first_inv = layer_norm(stream, first_gain, first_bias)
    normed = normed.astype(jnp.bfloat16)
    projected = matmul(normed, qkv_weight)
    shape_heads = (images, length, head_count, HEAD_DIM)
    queries = (
        (projected[..., :model_width] + query_bias.astype(jnp.float32))
        .astype(jnp.bfloat16)
        .reshape(shape_heads)
    )
    key_rows = (
        projected[..., model_width : 2 * model_width].astype(jnp.bfloat16).reshape(shape_heads)
    )
    values = (
        (projected[..., 2 * model_width :] + value_bias.astype(jnp.float32))
        .astype(jnp.bfloat16)
        .reshape(shape_heads)
    )
    scores = batched("bqhd,bkhd->bhqk", queries, key_rows) * score_scale
    log_total = jnp.log(jnp.sum(jnp.exp(scores), axis=-1, keepdims=True))
    weights = jnp.exp(scores - log_total).astype(jnp.bfloat16)
    attended = (
        batched("bhqk,bkhd->bqhd", weights, values)
        .reshape(images, length, model_width)
        .astype(jnp.bfloat16)
    )
    middle = stream + matmul(attended, out_weight) + out_bias.astype(jnp.float32)
    second_normed, second_hat, second_inv = layer_norm(middle, second_gain, second_bias)
    second_normed = second_normed.astype(jnp.bfloat16)
    hidden_pre = matmul(second_normed, up_weight) + up_bias.astype(jnp.float32)
    normal_cdf = 0.5 * (1.0 + lax.erf(hidden_pre * root_half))
    hidden = (hidden_pre * normal_cdf).astype(jnp.bfloat16)
    result = middle + matmul(hidden, down_weight) + down_bias.astype(jnp.float32)
    image_mask = live.astype(jnp.float32)[:, None, None]
    output = (result * image_mask).astype(jnp.bfloat16)
    saved = (
        normed,
        first_hat,
        first_inv,
        queries,
        key_rows,
        values,
        log_total,
        attended,
        second_normed,
        second_hat,
        second_inv,
        hidden_pre,
        normal_cdf,
        hidden,
        image_mask,
    )
    return (output, saved)


def backward_pass(params, saved, cotangent):
    (
        first_gain,
        first_bias,
        qkv_weight,
        query_bias,
        value_bias,
        out_weight,
        out_bias,
        second_gain,
        second_bias,
        up_weight,
        up_bias,
        down_weight,
        down_bias,
    ) = params
    (
        normed,
        first_hat,
        first_inv,
        queries,
        key_rows,
        values,
        log_total,
        attended,
        second_normed,
        second_hat,
        second_inv,
        hidden_pre,
        normal_cdf,
        hidden,
        image_mask,
    ) = saved
    images, length, head_count, head_width = queries.shape
    flat_shape = (images, length, head_count * head_width)
    score_scale = HEAD_DIM ** (-0.5)
    upstream = cotangent.astype(jnp.float32) * image_mask
    upstream_low = upstream.astype(jnp.bfloat16)
    down_weight_grad = outer_product(hidden, upstream_low)
    down_bias_grad = jnp.sum(upstream, axis=(0, 1))
    hidden_grad = matmul(upstream_low, down_weight.T)
    density = jnp.exp(-0.5 * hidden_pre * hidden_pre) * density_coef
    pre_grad = hidden_grad * (normal_cdf + hidden_pre * density)
    pre_low = pre_grad.astype(jnp.bfloat16)
    up_weight_grad = outer_product(second_normed, pre_low)
    up_bias_grad = jnp.sum(pre_grad, axis=(0, 1))
    second_in = matmul(pre_low, up_weight.T)
    second_gain_grad = jnp.sum(second_in * second_hat, axis=(0, 1))
    second_bias_grad = jnp.sum(second_in, axis=(0, 1))
    middle_grad = upstream + norm_back(second_in, second_hat, second_inv, second_gain)
    middle_low = middle_grad.astype(jnp.bfloat16)
    out_weight_grad = outer_product(attended, middle_low)
    out_bias_grad = jnp.sum(middle_grad, axis=(0, 1))
    attended_grad = matmul(middle_low, out_weight.T).astype(jnp.bfloat16).reshape(queries.shape)
    again_scores = batched("bqhd,bkhd->bhqk", queries, key_rows) * score_scale
    probs = jnp.exp(again_scores - log_total)
    probs_low = probs.astype(jnp.bfloat16)
    value_grad = batched("bhqk,bqhd->bkhd", probs_low, attended_grad)
    prob_grad = batched("bqhd,bkhd->bhqk", attended_grad, values)
    score_grad = (
        probs * (prob_grad - jnp.sum(probs * prob_grad, axis=-1, keepdims=True)) * score_scale
    ).astype(jnp.bfloat16)
    query_grad = batched("bhqk,bkhd->bqhd", score_grad, key_rows).reshape(flat_shape)
    key_grad = batched("bhqk,bqhd->bkhd", score_grad, queries).reshape(flat_shape)
    value_grad = value_grad.reshape(flat_shape)
    joined = jnp.concatenate([query_grad, key_grad, value_grad], axis=-1).astype(jnp.bfloat16)
    qkv_weight_grad = outer_product(normed, joined)
    query_bias_grad = jnp.sum(query_grad, axis=(0, 1))
    value_bias_grad = jnp.sum(value_grad, axis=(0, 1))
    first_in = matmul(joined, qkv_weight.T)
    first_gain_grad = jnp.sum(first_in * first_hat, axis=(0, 1))
    first_bias_grad = jnp.sum(first_in, axis=(0, 1))
    middle_grad = middle_grad + norm_back(first_in, first_hat, first_inv, first_gain)
    input_grad = middle_grad.astype(jnp.bfloat16)
    grads = (
        first_gain_grad,
        first_bias_grad,
        qkv_weight_grad,
        query_bias_grad,
        value_bias_grad,
        out_weight_grad,
        out_bias_grad,
        second_gain_grad,
        second_bias_grad,
        up_weight_grad,
        up_bias_grad,
        down_weight_grad,
        down_bias_grad,
    )
    return (input_grad, grads)


MESH = pl.DeviceIdType.MESH
def ring_index(position, n):
    half = position // (n // 2)
    return (1 - half) * 2 * position + half * (2 * (n - 1 - position) + 1)


def ring_position(index, n):
    odd = index % 2
    step = index // 2
    return (1 - odd) * step + odd * (n - 1 - step)


def places(n):
    rep = lax.axis_index("rep")
    me = lax.axis_index("shard")
    core = rep % 2
    row = rep // 2
    position = ring_position(me, n)
    right = (rep, ring_index((position + 1) % n, n))
    left = (rep, ring_index((position + n - 1) % n, n))
    partner = (row * 2 + 1 - core, me)
    across = ((1 - row) * 2 + core, me)
    return me, core, row, position, right, left, partner, across


def greet(peers):
    barrier = pltpu.get_barrier_semaphore()
    for peer in peers:
        pl.semaphore_signal(barrier, inc=1, device_id=peer, device_id_type=MESH)
    pl.semaphore_wait(barrier, len(peers))


def remote(source, target, send, recv, device):
    return pltpu.make_async_remote_copy(
        src_ref=source,
        dst_ref=target,
        send_sem=send,
        recv_sem=recv,
        device_id=device,
        device_id_type=MESH,
    )


def window(refs, side, part, block, width):
    qkv, out, up, down = refs
    if side == 2:
        return [(None, down.at[block, part])]
    if side == 1:
        return [(None, up.at[block, :, pl.ds(pl.multiple_of(part * width, width), width)])]
    inner = part - part // 3
    return [
        (part < 3, qkv.at[block, :, pl.ds(pl.multiple_of(inner * width, width), width)]),
        (part == 3, out.at[block]),
    ]


def start_each(views, make):
    for condition, view in views:
        if condition is None:
            make(view).start()
        else:
            pl.when(condition)(make(view).start)


def gather_kernel(
    n,
    width,
    qkv_in,
    out_in,
    up_in,
    down_in,
    line_in,
    qkv_ref,
    out_ref,
    up_ref,
    down_ref,
    line_ref,
    local_sem,
    ring_s,
    ring_r,
    core_s,
    core_r,
    row_s,
    row_r,
    last_s,
    last_r,
    line_s,
    line_r,
):
    me, core, row, position, right, left, partner, across = places(n)
    refs = (qkv_ref, out_ref, up_ref, down_ref)
    pairs = zip((qkv_in, out_in, up_in, down_in, line_in), refs + (line_ref,))
    locals_ = [
        pltpu.make_async_copy(source, target.at[me], local_sem.at[i])
        for i, (source, target) in enumerate(pairs)
    ]
    for copy in locals_:
        copy.start()
    greet((right, left, partner, across))
    for copy in locals_:
        copy.wait()

    def block(way, r):
        return ring_index((position + (1 if way else n - 1) * r) % n, n)

    def views(i, r, whose):
        way, kind = i // 2, i % 2
        side, part = (2, 2 * whose + way) if kind else (way, 2 * whose + row)
        return window(refs, side, part, block(way, r), width)

    def over(way, r, whose):
        return window(refs, way, 2 * whose + 1 - row, block(way, r), width)

    def ring(i, r):
        peer = left if i // 2 else right
        return lambda v: remote(v, v, ring_s.at[i, r], ring_r.at[i, r], peer)

    def to_core(i, r):
        return lambda v: remote(v, v, core_s.at[i, r], core_r.at[i, r], partner)

    def to_row(way, r):
        return lambda v: remote(v, v, row_s.at[way, r], row_r.at[way, r], across)

    def to_last(way, r):
        return lambda v: remote(v, v, last_s.at[way, r], last_r.at[way, r], partner)

    def line(r):
        view = line_ref.at[block(0, r)]
        return remote(view, view, line_s.at[r], line_r.at[r], right)

    def one(vs):
        return vs[0][1]

    for i in range(4):
        start_each(views(i, 0, core), ring(i, 0))
    line(0).start()

    def relay(r):
        for way in range(2):
            to_row(way, r)(one(over(way, r + 1, core))).wait_recv()
            start_each(over(way, r + 1, core), to_last(way, r))

    def step(r, carry):
        for i in (0, 2, 1, 3):
            got = views(i, r + 1, core)
            ring(i, r)(one(got)).wait_recv()

            @pl.when(r < n - 2)
            def _():
                start_each(got, ring(i, r + 1))

            if i % 2 == 0:
                start_each(got, to_row(i // 2, r))
            start_each(got, to_core(i, r))
        line(r).wait_recv()

        @pl.when(r < n - 2)
        def _():
            line(r + 1).start()

        @pl.when(r > 0)
        def _():
            relay(r - 1)

        return carry

    lax.fori_loop(0, n - 1, step, 0)
    relay(n - 2)

    def finish(r, carry):
        for i in range(4):
            view = one(views(i, r, core))
            ring(i, r)(view).wait_send()
            to_core(i, r)(view).wait_send()
            to_core(i, r)(view).wait_recv()
        for way in range(2):
            view = one(views(2 * way, r, core))
            to_row(way, r)(view).wait_send()
            to_last(way, r)(view).wait_send()
            to_last(way, r)(view).wait_recv()
        line(r).wait_send()
        return carry

    lax.fori_loop(0, n - 1, finish, 0)


def gather_all(arrays, n, width):
    dma = pltpu.SemaphoreType.DMA
    return pl.pallas_call(
        functools.partial(gather_kernel, n, width),
        out_shape=[jax.ShapeDtypeStruct((n,) + a.shape, a.dtype) for a in arrays],
        in_specs=[pl.BlockSpec(memory_space=pltpu.VMEM)] * len(arrays),
        out_specs=[pl.BlockSpec(memory_space=pl.ANY)] * len(arrays),
        scratch_shapes=[dma((len(arrays),))]
        + [dma((4, n - 1))] * 4
        + [dma((2, n - 1))] * 4
        + [dma((n - 1,))] * 2,
        compiler_params=pltpu.CompilerParams(collective_id=0, has_side_effects=True),
        name="gather_all",
    )(*arrays)


def reduce_kernel(
    n,
    width,
    qkv_ref,
    out_ref,
    up_ref,
    down_ref,
    line_ref,
    sums,
    line_out,
    own,
    given,
    arrive,
    over,
    other,
    line_send,
    line_got,
    line_pair,
    own_sem,
    given_s,
    given_r,
    ring_s,
    ring_r,
    row_s,
    row_r,
    end_row_s,
    end_row_r,
    end_core_s,
    end_core_r,
    line_s,
    line_r,
    pair_s,
    pair_r,
):
    me, core, row, position, right, left, partner, across = places(n)
    refs = (qkv_ref, out_ref, up_ref, down_ref)
    f32 = jnp.float32

    def block(way, k):
        return ring_index((position + (1 if way else n - 1) * (k + 1)) % n, n)

    def source(i, k, whose):
        way, kind = i % 2, i // 2
        side, part = (
            (way, 2 * whose + row),
            (2, 2 * whose + way),
            (way, 2 * whose + 1 - row),
        )[kind]
        return window(refs, side, part, block(way, k), width)

    def load(i, k):
        return lambda v: pltpu.make_async_copy(v, own.at[i, k], own_sem.at[i, k])

    def give(i, k):
        return lambda v: remote(v, given.at[i, k], given_s.at[i, k], given_r.at[i, k], partner)

    def ring(i, k):
        peer = left if i % 2 else right
        return remote(own.at[i, k], arrive.at[i, k], ring_s.at[i, k], ring_r.at[i, k], peer)

    def to_row(way, k):
        return remote(
            own.at[4 + way, k], over.at[way, k], row_s.at[way, k], row_r.at[way, k], across
        )

    def line_ring(k):
        return remote(line_send.at[k], line_got.at[k], line_s.at[k], line_r.at[k], right)

    order = (4, 5, 2, 3, 0, 1)

    def loads(k, carry):
        for i in order:
            start_each(source(i, k, core), load(i, k))
        return carry

    lax.fori_loop(0, n, loads, 0)
    greet((right, left, partner, across))

    def gives(k, carry):
        for i in order:
            start_each(source(i, k, 1 - core), give(i, k))
        return carry

    lax.fori_loop(0, n, gives, 0)

    def take(i, k):
        view = source(i, k, core)[0][1]
        load(i, k)(view).wait()
        give(i, k)(view).wait_recv()
        return own[i, k].astype(f32) + given[i, k].astype(f32)

    def put(i, k, total):
        own[i, k] = total.astype(own.dtype)

    def ahead(k):
        for way in range(2):
            put(4 + way, k, take(4 + way, k))
            to_row(way, k).start()

    def partial(i, k, first):
        total = take(i, k)
        if i < 2:
            to_row(i, k).wait_recv()
            total = total + over[i, k].astype(f32)
        if not first:
            ring(i, k - 1).wait_recv()
            total = total + arrive[i, k - 1].astype(f32)
        return total

    ahead(0)
    line_send[0] = line_ref[block(0, 0)]
    line_ring(0).start()
    ahead(1)
    for i in (2, 3, 0, 1):
        put(i, 0, partial(i, 0, True))
        ring(i, 0).start()

    def step(k, carry):
        ahead(k + 1)
        for i in (2, 3, 0, 1):
            put(i, k, partial(i, k, False))
            ring(i, k).start()
        line_ring(k - 1).wait_recv()
        line_send[k] = line_ref[block(0, k)] + line_got[k - 1]
        line_ring(k).start()
        return carry

    lax.fori_loop(1, n - 1, step, 0)

    def end_row(i, k=None):
        if i < 2:
            view = sums.at[i, 2 * core + row]
            return remote(view, view, end_row_s.at[i], end_row_r.at[i], across)
        return remote(
            own.at[i, n - 1], other.at[i - 2], end_row_s.at[i], end_row_r.at[i], across
        )

    def end_core(j, side, part):
        view = sums.at[side, part]
        return remote(view, view, end_core_s.at[j], end_core_r.at[j], partner)

    for i in (2, 3):
        put(i, n - 1, partial(i, n - 1, False))
        end_row(i).start()
    line_ring(n - 2).wait_recv()
    line_pair[0] = line_ref[me] + line_got[n - 2]
    pair_row = remote(line_pair.at[0], line_pair.at[1], pair_s.at[0], pair_r.at[0], across)
    pair_row.start()
    for way in (0, 1):
        sums[way, 2 * core + row] = partial(way, n - 1, False).astype(sums.dtype)
        end_row(way).start()
        end_core(way, way, 2 * core + row).start()
    pair_row.wait()
    line_pair[2] = line_pair[0] + line_pair[1]
    pair_core = remote(line_pair.at[2], line_pair.at[3], pair_s.at[1], pair_r.at[1], partner)
    pair_core.start()
    for way in (0, 1):
        end_row(2 + way).wait_recv()
        total = own[2 + way, n - 1].astype(f32) + other[way].astype(f32)
        sums[2, 2 * core + way] = total.astype(sums.dtype)
        end_core(2 + way, 2, 2 * core + way).start()
    for way in (0, 1):
        end_row(way).wait_recv()
        end_core(4 + way, way, 2 * core + 1 - row).start()
    pair_core.wait()
    line_out[...] = line_pair[2] + line_pair[3]
    for i in range(4):
        end_row(i).wait_send()
    for j in range(6):
        copy = end_core(j, 0, 0)
        copy.wait_send()
        copy.wait_recv()

    def finish(k, carry):
        for i in range(6):
            give(i, k)(source(i, k, core)[0][1]).wait_send()
        for way in range(2):
            to_row(way, k).wait_send()
        return carry

    lax.fori_loop(0, n, finish, 0)

    def finish_ring(k, carry):
        for i in range(4):
            ring(i, k).wait_send()
        line_ring(k).wait_send()
        return carry

    lax.fori_loop(0, n - 1, finish_ring, 0)


def reduce_all(arrays, n, width):
    dma = pltpu.SemaphoreType.DMA
    vmem = pltpu.VMEM
    rows = arrays[0].shape[1]
    low = arrays[0].dtype
    line = arrays[-1].shape[1:]
    anywhere = pl.BlockSpec(memory_space=pl.ANY)
    near = pl.BlockSpec(memory_space=pltpu.VMEM)
    return pl.pallas_call(
        functools.partial(reduce_kernel, n, width),
        out_shape=[
            jax.ShapeDtypeStruct((3, 4, rows, width), low),
            jax.ShapeDtypeStruct(line, jnp.float32),
        ],
        in_specs=[anywhere] * 4 + [near],
        out_specs=[near, near],
        scratch_shapes=[
            vmem((6, n, rows, width), low),
            vmem((6, n, rows, width), low),
            vmem((4, n - 1, rows, width), low),
            vmem((2, n, rows, width), low),
            vmem((2, rows, width), low),
            vmem((n - 1,) + line, jnp.float32),
            vmem((n - 1,) + line, jnp.float32),
            vmem((4,) + line, jnp.float32),
            dma((6, n)),
            dma((6, n)),
            dma((6, n)),
            dma((4, n - 1)),
            dma((4, n - 1)),
            dma((2, n)),
            dma((2, n)),
            dma((4,)),
            dma((4,)),
            dma((6,)),
            dma((6,)),
            dma((n - 1,)),
            dma((n - 1,)),
            dma((2,)),
            dma((2,)),
        ],
        compiler_params=pltpu.CompilerParams(
            collective_id=1, has_side_effects=True, vmem_limit_bytes=56 * 1024 * 1024
        ),
        name="reduce_all",
    )(*arrays)


LANES = 128


def per_device(n, layer_input, cotangent, live, *params):
    width = params[0].shape[0] * n
    rows = params[0].shape[0]
    matrices = [i for i, p in enumerate(params) if p.ndim == 2]
    vectors = [i for i, p in enumerate(params) if p.ndim == 1]
    shapes = [params[i].shape for i in matrices]
    assert shapes == [(rows, 3 * width), (rows, width), (rows, 4 * width), (4 * rows, width)]
    lengths = [params[i].shape[0] for i in vectors]
    tall = -(-sum(lengths) // (16 * LANES)) * 16
    spare = tall * LANES - sum(lengths)

    line = jnp.concatenate([params[i] for i in vectors] + [jnp.zeros(spare, params[0].dtype)])
    sent = [params[i] for i in matrices]
    sent[3] = sent[3].reshape(4, rows, width)
    *full, lines = gather_all(sent + [line.reshape(tall, LANES)], n, width)
    gathered = [None] * len(params)
    for i, array in zip(matrices, full):
        gathered[i] = array.reshape(n * params[i].shape[0], params[i].shape[1])
    tail = lines.reshape(n, -1)
    at = 0
    for i, length in zip(vectors, lengths):
        gathered[i] = tail[:, at : at + length].reshape(-1)
        at += length

    output, saved = forward_pass(gathered, layer_input, live)
    input_grad, grads = backward_pass(gathered, saved, cotangent)

    low = jnp.bfloat16
    blocks = [grads[i].astype(low).reshape((n,) + a.shape) for i, a in zip(matrices, sent)]
    parts = [grads[i].reshape(n, -1) for i in vectors] + [jnp.zeros((n, spare), jnp.float32)]
    blocks.append(jnp.concatenate(parts, axis=1).reshape(n, tall, LANES))
    sums, tail = reduce_all(blocks, n, width)

    def joined(pieces):
        return jnp.swapaxes(pieces, 0, 1).reshape(rows, -1).astype(jnp.float32)

    results = [None] * len(params)
    whole = (
        joined(sums[0, :3]),
        sums[0, 3].astype(jnp.float32),
        joined(sums[1]),
        sums[2].reshape(4 * rows, width).astype(jnp.float32),
    )
    for i, array in zip(matrices, whole):
        results[i] = array
    tail = tail.reshape(-1)
    at = 0
    for i, length in zip(vectors, lengths):
        results[i] = tail[at : at + length]
        at += length
    return (output, input_grad, *results)


def solution(mesh):
    placed = (
        P(("rep", "shard"), None, None),
        P(("rep", "shard"), None, None),
        P(("rep", "shard")),
        P("shard"),
        P("shard"),
        P("shard", None),
        P("shard"),
        P("shard"),
        P("shard", None),
        P("shard"),
        P("shard"),
        P("shard"),
        P("shard", None),
        P("shard"),
        P("shard", None),
        P("shard"),
    )
    return jax.shard_map(
        functools.partial(per_device, mesh.shape["shard"]),
        mesh=mesh,
        in_specs=placed,
        out_specs=(
            P(("rep", "shard"), None, None),
            P(("rep", "shard"), None, None),
            P("shard"),
            P("shard"),
            P("shard", None),
            P("shard"),
            P("shard"),
            P("shard", None),
            P("shard"),
            P("shard"),
            P("shard"),
            P("shard", None),
            P("shard"),
            P("shard", None),
            P("shard"),
        ),
        check_vma=False,
    )
```
